32 devices in a mesh: row: 8 (over z, core), col: 4 (over y, x).
Axes of the slice: x: 2, y: 2, z: 4, core: 2. Of those that a mesh axis runs over, the one named last changes fastest.
Arguments:
- features: bfloat16 [8, 4, 1024, 602], P('row', 'col'), may hold values from -6 to 6
- local_mask: int32 [8, 4, 1024, 1024], P('row', 'col'), may hold values 0 or 1
- halo_mask: int32 [8, 4, 1024, 512], P('row', 'col'), may hold values 0 or 1
- boundary_index: int32 [8, 4, 512], P('row', 'col'), may hold values from 0 to 1023
- labels: int32 [8, 4, 1024], P('row', 'col'), may hold values from 0 to 40
- halo_first: bfloat16 [8, 4, 512, 602], P('row', 'col'), may hold values from -6 to 6
- halo_second: bfloat16 [8, 4, 512, 256], P('row', 'col'), may hold values from -4 to 4
- halo_third: bfloat16 [8, 4, 512, 256], P('row', 'col'), may hold values from -4 to 4
- return_second: bfloat16 [8, 4, 512, 256], P('row', 'col'), may hold values from -0.0059814453 to 0.0059814453
- return_third: bfloat16 [8, 4, 512, 256], P('row', 'col'), may hold values from -0.0059814453 to 0.0059814453
- weight_first: bfloat16 [602, 256], replicated, may hold values from -1 to 1
- weight_second: bfloat16 [256, 256], replicated, may hold values from -1.5 to 1.5
- weight_third: bfloat16 [256, 41], replicated, may hold values from -1.5 to 1.5
Outputs:
- grad_first: float32 [602, 256], replicated
- grad_second: float32 [256, 256], replicated
- grad_third: float32 [256, 41], replicated
- next_second: bfloat16 [8, 4, 512, 256], P('row', 'col')
- next_third: bfloat16 [8, 4, 512, 256], P('row', 'col')
- back_second: bfloat16 [8, 4, 512, 256], P('row', 'col')
- back_third: bfloat16 [8, 4, 512, 256], P('row', 'col')
The draws below stay inside these ranges and needn't reach their ends.
All inputs are finite; a program needn't handle non-finite values. No bound on the sum of `local_mask` or of `halo_mask` on one device may be relied on, other than what follows from the above.
Results may differ from the reference program's by a relative error of at most 0.007.
Values may be sent and summed in bfloat16 or wider, within the bound.
A program may use at most 64 MiB of HBM per device.

```python
import jax
import jax.numpy as jnp
from jax import lax

IN_DIM = 602
HIDDEN_SIZE = 256
CLASSES = 41
NODE_DEV = 1024
BOUND = 128
N_ROW = 8
N_COL = 4


def place_ends(drawn, key, smallest, top_value):
    index_at = [jax.random.randint(jax.random.fold_in(key, axis), (), 0, length) for axis, length in enumerate(drawn.shape)]
    widest = drawn.shape.index(max(drawn.shape))
    neighbour = index_at[:widest] + [(index_at[widest] + 1) % drawn.shape[widest]] + index_at[widest + 1:]
    return drawn.at[tuple(index_at)].set(smallest).at[tuple(neighbour)].set(top_value)


def level_of(rng, dims, cuts, smallest, top_value):
    def one(dim, blocks):
        steps = jax.random.uniform(jax.random.fold_in(jax.random.fold_in(rng, 6), dim), (blocks,), jnp.float32, smallest / len(cuts), top_value / len(cuts))
        return jnp.repeat(jnp.exp(steps), dims[dim] // blocks).reshape((-1,) + (1,) * (len(dims) - dim - 1))

    level = one(*cuts[0])
    for cut in cuts[1:]:
        level = level * one(*cut)
    return level


def bell_draw(rng, dims, scale, bound, cuts=(), held_as=jnp.bfloat16):
    entries = scale * jax.random.normal(rng, dims, jnp.float32)
    if cuts:
        entries = entries * level_of(rng, dims, cuts, -0.22, 0.18)
    return jnp.clip(entries, -bound, bound).astype(held_as)


def setup_inputs(seed: int = 0) -> dict:
    keys = jax.random.split(jax.random.key(seed), 14)
    return {
        "features": bell_draw(keys[0], (N_ROW, N_COL, NODE_DEV, IN_DIM), 1.0, 6.0, ((0, 8), (1, 4))),
        "local_mask": place_ends((jax.random.randint(keys[1], (N_ROW, N_COL, NODE_DEV, NODE_DEV), 0, NODE_DEV) < min(16, NODE_DEV // 4)).astype(jnp.int32), jax.random.fold_in(keys[1], 1), 0, 1),
        "halo_mask": place_ends((jax.random.randint(keys[2], (N_ROW, N_COL, NODE_DEV, 4 * BOUND), 0, BOUND) < min(2, BOUND // 4)).astype(jnp.int32), jax.random.fold_in(keys[2], 1), 0, 1),
        "boundary_index": place_ends(jax.random.randint(keys[3], (N_ROW, N_COL, 4 * BOUND), 0, NODE_DEV), jax.random.fold_in(keys[3], 1), 0, NODE_DEV - 1).astype(jnp.int32),
        "labels": place_ends(jax.random.randint(keys[4], (N_ROW, N_COL, NODE_DEV), 0, CLASSES), jax.random.fold_in(keys[4], 1), 0, CLASSES - 1).astype(jnp.int32),
        "halo_first": bell_draw(keys[5], (N_ROW, N_COL, 4 * BOUND, IN_DIM), 1.0, 6.0, ((0, 8), (1, 4))),
        "halo_second": bell_draw(keys[6], (N_ROW, N_COL, 4 * BOUND, HIDDEN_SIZE), 0.5, 4.0, ((0, 8), (1, 4))),
        "halo_third": bell_draw(keys[7], (N_ROW, N_COL, 4 * BOUND, HIDDEN_SIZE), 0.5, 4.0, ((0, 8), (1, 4))),
        "return_second": bell_draw(keys[8], (N_ROW, N_COL, 4 * BOUND, HIDDEN_SIZE), 0.001, 0.0059814453, ((0, 8), (1, 4))),
        "return_third": bell_draw(keys[9], (N_ROW, N_COL, 4 * BOUND, HIDDEN_SIZE), 0.001, 0.0059814453, ((0, 8), (1, 4))),
        "weight_first": bell_draw(keys[10], (IN_DIM, HIDDEN_SIZE), (IN_DIM // 16) ** -0.5, 1.0),
        "weight_second": bell_draw(keys[11], (HIDDEN_SIZE, HIDDEN_SIZE), (HIDDEN_SIZE // 16) ** -0.5, 1.5),
        "weight_third": bell_draw(keys[12], (HIDDEN_SIZE, CLASSES), (HIDDEN_SIZE // 16) ** -0.5, 1.5),
    }


def slope(pre):
    sigma = jax.nn.sigmoid(pre)
    return sigma * (1.0 + pre * (1.0 - sigma))


def spread(local_bf, halo_bf, inverse, values, remote):
    summed = jnp.dot(local_bf, values, preferred_element_type=jnp.float32)
    summed = summed + values.astype(jnp.float32)
    summed = summed + jnp.dot(halo_bf, remote, preferred_element_type=jnp.float32)
    return (summed * inverse).astype(jnp.bfloat16)


def retract(local_bf, halo_bf, inverse, upstream, weight, hits, returned):
    across = jnp.dot(upstream, weight.T, preferred_element_type=jnp.float32)
    scaled = (across * inverse).astype(jnp.bfloat16)
    carried = jnp.dot(local_bf.T, scaled, preferred_element_type=jnp.float32) + scaled.astype(jnp.float32)
    carried = carried + jnp.dot(hits, returned, preferred_element_type=jnp.float32)
    outgoing = jnp.dot(halo_bf.T, scaled, preferred_element_type=jnp.float32).astype(jnp.bfloat16)
    return carried, outgoing


def partition(features, local_mask, halo_mask, boundary_index, labels, halo_first, halo_second, halo_third,
              return_second, return_third, weight_first, weight_second, weight_third):
    local_bf = local_mask.astype(jnp.bfloat16)
    halo_bf = halo_mask.astype(jnp.bfloat16)
    degree = 1.0 + jnp.sum(local_mask, axis=1).astype(jnp.float32) + jnp.sum(halo_mask, axis=1).astype(jnp.float32)
    inverse = (1.0 / degree)[:, None]
    node_rows = features.shape[0]
    hits = (jnp.arange(node_rows, dtype=jnp.int32)[:, None] == boundary_index[None, :]).astype(jnp.bfloat16)
    mixed_one = spread(local_bf, halo_bf, inverse, features, halo_first)
    pre_one = jnp.dot(mixed_one, weight_first, preferred_element_type=jnp.float32)
    hidden_one = jax.nn.silu(pre_one).astype(jnp.bfloat16)
    mixed_two = spread(local_bf, halo_bf, inverse, hidden_one, halo_second)
    pre_two = jnp.dot(mixed_two, weight_second, preferred_element_type=jnp.float32)
    hidden_two = jax.nn.silu(pre_two).astype(jnp.bfloat16)
    mixed_three = spread(local_bf, halo_bf, inverse, hidden_two, halo_third)
    logits = jnp.dot(mixed_three, weight_third, preferred_element_type=jnp.float32)
    expo = jnp.exp(logits)
    probs = expo / jnp.sum(expo, axis=1, keepdims=True)
    target = (labels[:, None] == jnp.arange(logits.shape[1], dtype=jnp.int32)[None, :]).astype(jnp.float32)
    upstream_three = ((probs - target) / node_rows).astype(jnp.bfloat16)
    grad_three = jnp.dot(mixed_three.T, upstream_three, preferred_element_type=jnp.float32)
    carried_two, outgoing_three = retract(local_bf, halo_bf, inverse, upstream_three, weight_third, hits, return_third)
    upstream_two = (carried_two * slope(pre_two)).astype(jnp.bfloat16)
    grad_two = jnp.dot(mixed_two.T, upstream_two, preferred_element_type=jnp.float32)
    carried_one, outgoing_two = retract(local_bf, halo_bf, inverse, upstream_two, weight_second, hits, return_second)
    upstream_one = (carried_one * slope(pre_one)).astype(jnp.bfloat16)
    grad_one = jnp.dot(mixed_one.T, upstream_one, preferred_element_type=jnp.float32)
    sent_second = jnp.take(hidden_one, boundary_index, axis=0)
    sent_third = jnp.take(hidden_two, boundary_index, axis=0)
    return grad_one, grad_two, grad_three, sent_second, sent_third, outgoing_two, outgoing_three


def route(sent):
    parted = sent.reshape((N_ROW, N_COL, 4, BOUND, sent.shape[-1]))
    blank_row = jnp.zeros_like(parted[:1, :, 0])
    blank_col = jnp.zeros_like(parted[:, :1, 0])
    from_above = jnp.concatenate([blank_row, parted[:-1, :, 1]], axis=0)
    from_below = jnp.concatenate([parted[1:, :, 0], blank_row], axis=0)
    from_left = jnp.concatenate([blank_col, parted[:, :-1, 3]], axis=1)
    from_right = jnp.concatenate([parted[:, 1:, 2], blank_col], axis=1)
    return jnp.stack([from_above, from_below, from_left, from_right], axis=2).reshape(sent.shape)


def reference(features, local_mask, halo_mask, boundary_index, labels, halo_first, halo_second, halo_third,
              return_second, return_third, weight_first, weight_second, weight_third):
    partitions = N_ROW * N_COL

    def flatten(array):
        return array.reshape((partitions,) + array.shape[2:])

    def advance(totals, pieces):
        result = partition(*pieces, weight_first, weight_second, weight_third)
        return (totals[0] + result[0], totals[1] + result[1], totals[2] + result[2]), result[3:]

    start = (jnp.zeros(weight_first.shape, jnp.float32), jnp.zeros(weight_second.shape, jnp.float32),
             jnp.zeros(weight_third.shape, jnp.float32))
    inputs = tuple(flatten(array) for array in (features, local_mask, halo_mask, boundary_index, labels, halo_first,
                                                halo_second, halo_third, return_second, return_third))
    sums, sends = lax.scan(advance, start, inputs)
    shaped = [route(piece.reshape((N_ROW, N_COL) + piece.shape[1:])) for piece in sends]
    return sums[0], sums[1], sums[2], shaped[0], shaped[1], shaped[2], shaped[3]
```

```python
import functools

import jax
import jax.numpy as jnp
from jax import lax
from jax.experimental import pallas as pl
from jax.experimental.pallas import tpu as pltpu
from jax.sharding import PartitionSpec as P

MESH = pl.DeviceIdType.MESH
BF = jnp.bfloat16
F32 = jnp.float32


def up_to(value, step):
    return -(-value // step) * step


def dot(a, b, dims=((1,), (0,))):
    return lax.dot_general(a, b, (dims, ((), ())), preferred_element_type=F32)


def slope(pre):
    sigma = jax.nn.sigmoid(pre)
    return sigma * (1.0 + pre * (1.0 - sigma))


class Plan:
    def __init__(self, mesh, rows, width):
        self.n_row, self.n_col = mesh.shape["row"], mesh.shape["col"]
        self.pair = 2 if self.n_row % 2 == 0 else 1
        self.deep = self.n_row // self.pair
        self.offsets, at = [], 0
        for count in rows:
            self.offsets.append(at)
            at = up_to(at + count, 16)
        self.small = up_to(up_to(at, 16) // 16, self.n_row * self.n_col) * 16 // (self.n_row * self.n_col)
        self.quarter = self.small * self.deep
        self.half = self.quarter * self.n_col
        self.total = self.half * self.pair
        self.width = width

    def place(self):
        self.r, self.c = lax.axis_index("row"), lax.axis_index("col")
        self.core, self.z = self.r % self.pair, self.r // self.pair
        self.mate = self.r + 1 - 2 * self.core

    def col_peer(self, d):
        return (self.c + d) % self.n_col

    def deep_peer(self, d):
        return (self.z + d) % self.deep

    def deep_id(self, d):
        return (self.deep_peer(d) * self.pair + self.core, self.c)

    def greet(self):
        barrier = pltpu.get_barrier_semaphore()

        def hello(device):
            pl.semaphore_signal(barrier, inc=1, device_id=device, device_id_type=MESH)

        count = 0
        if self.pair == 2:
            hello((self.mate, self.c))
            count += 1
        for d in range(1, self.n_col):
            hello((self.r, self.col_peer(d)))
            count += 1
        for d in range(1, self.deep):
            hello(self.deep_id(d))
            count += 1
        for step, there in self.far_rows():
            @pl.when(there)
            def _():
                hello((self.r + step, self.c))
        for _, there in self.far_rows():
            count = count + jnp.where(there, 1, 0)
        pl.semaphore_wait(barrier, count)

    def far_rows(self):
        if self.pair == 2:
            return ((-1, jnp.logical_and(self.core == 0, self.r > 0)),
                    (1, jnp.logical_and(self.core == 1, self.r < self.n_row - 1)))
        return ()

    def edges(self):
        r, c = self.r, self.c
        return (((r - 1, c), 1, r > 0), ((r + 1, c), 0, r < self.n_row - 1),
                ((r, c - 1), 3, c > 0), ((r, c + 1), 2, c < self.n_col - 1))


def rows_at(start, count):
    return pl.ds(pl.multiple_of(start, 16), count)


def halo_copy(plan, k, src, dst, send, recv, way):
    bound = src.shape[0] // 4
    device, slot, there = plan.edges()[k]
    copy = pltpu.make_async_remote_copy(
        src_ref=src.at[pl.ds(k * bound, bound)], dst_ref=dst.at[pl.ds(slot * bound, bound)],
        send_sem=send.at[way, k], recv_sem=recv.at[way, slot], device_id=device, device_id_type=MESH)
    return copy, slot, there


def halo_start(plan, src, dst, send, recv, way):
    bound = src.shape[0] // 4
    for k in range(4):
        copy, _, there = halo_copy(plan, k, src, dst, send, recv, way)

        @pl.when(there)
        def _():
            copy.start()

        @pl.when(jnp.logical_not(there))
        def _():
            dst[pl.ds(k * bound, bound), :] = jnp.zeros((bound, dst.shape[1]), dst.dtype)


def halo_finish(plan, src, dst, send, recv, way):
    bound = src.shape[0] // 4
    for k in range(4):
        copy, _, there = halo_copy(plan, k, src, dst, send, recv, way)
        arrival = pltpu.make_async_remote_copy(
            src_ref=src.at[pl.ds(k * bound, bound)], dst_ref=dst.at[pl.ds(k * bound, bound)],
            send_sem=send.at[way, k], recv_sem=recv.at[way, k], device_id=plan.edges()[k][0], device_id_type=MESH)

        @pl.when(there)
        def _():
            copy.wait_send()
            arrival.wait_recv()


def reduce_all(plan, packed, packed_bf, got_pair, got_col, got_deep, acc_bf, whole, sems):
    pair_s, pair_r, col_s, col_r, deep_s, deep_r, gdeep_s, gdeep_r, gcol_s, gcol_r, gpair_s, gpair_r = sems
    half, quarter, small = plan.half, plan.quarter, plan.small

    def remote(src, dst, s, r, device):
        return pltpu.make_async_remote_copy(src_ref=src, dst_ref=dst, send_sem=s, recv_sem=r,
                                            device_id=device, device_id_type=MESH)

    mine = plan.core * half
    if plan.pair == 2:
        first = remote(packed_bf.at[rows_at((1 - plan.core) * half, half)], got_pair, pair_s, pair_r, (plan.mate, plan.c))
        first.start()
        first.wait()
        summed = packed[rows_at(mine, half), :] + got_pair[...].astype(F32)
    else:
        summed = packed[rows_at(mine, half), :]
    packed[rows_at(mine, half), :] = summed
    acc_bf[...] = summed.astype(BF)
    copies = []
    for d in range(1, plan.n_col):
        peer = plan.col_peer(d)
        copies.append(remote(acc_bf.at[rows_at(peer * quarter, quarter)], got_col.at[d - 1], col_s.at[d - 1], col_r.at[d - 1], (plan.r, peer)))
        copies[-1].start()
    own = mine + plan.c * quarter
    total = packed[rows_at(own, quarter), :]
    for d, copy in enumerate(copies):
        copy.wait()
        total = total + got_col[d].astype(F32)
    packed[rows_at(own, quarter), :] = total
    acc_bf[0:quarter, :] = total.astype(BF)
    copies = []
    for d in range(1, plan.deep):
        peer = plan.deep_peer(d)
        copies.append(remote(acc_bf.at[rows_at(peer * small, small)], got_deep.at[d - 1], deep_s.at[d - 1], deep_r.at[d - 1], plan.deep_id(d)))
        copies[-1].start()
    last = own + plan.z * small
    total = packed[rows_at(last, small), :]
    for d, copy in enumerate(copies):
        copy.wait()
        total = total + got_deep[d].astype(F32)
    whole[rows_at(last, small), :] = total.astype(BF)
    copies = []
    for d in range(1, plan.deep):
        part = whole.at[rows_at(last, small)]
        copies.append(remote(part, part, gdeep_s.at[d - 1], gdeep_r.at[d - 1], plan.deep_id(d)))
        copies[-1].start()
    for copy in copies:
        copy.wait()
    copies = []
    for d in range(1, plan.n_col):
        part = whole.at[rows_at(own, quarter)]
        copies.append(remote(part, part, gcol_s.at[d - 1], gcol_r.at[d - 1], (plan.r, plan.col_peer(d))))
        copies[-1].start()
    for copy in copies:
        copy.wait()
    if plan.pair == 2:
        part = whole.at[rows_at(mine, half)]
        final = remote(part, part, gpair_s, gpair_r, (plan.mate, plan.c))
        final.start()
        final.wait()


def traffic(plan, g1, g2, g3, s2, s3, o2, o3, out1, out2, out3, n2, n3, b2, b3,
            packed, packed_bf, got_pair, got_col, got_deep, acc_bf, whole, hsend, hrecv, *sems):
    plan.place()
    plan.greet()
    packed[...] = jnp.zeros_like(packed)
    for ref, at in zip((g1, g2, g3), plan.offsets):
        packed[at:at + ref.shape[0], :] = ref[...]
    packed_bf[...] = packed[...].astype(BF)
    trades = ((s2, n2), (s3, n3), (o3, b3), (o2, b2))
    for way, (src, dst) in enumerate(trades):
        halo_start(plan, src, dst, hsend, hrecv, way)
    reduce_all(plan, packed, packed_bf, got_pair, got_col, got_deep, acc_bf, whole, sems)
    for ref, at in zip((out1, out2, out3), plan.offsets):
        ref[...] = whole[at:at + ref.shape[0], :].astype(F32)
    for way, (src, dst) in enumerate(trades):
        halo_finish(plan, src, dst, hsend, hrecv, way)


def comm_scratch(plan):
    width = plan.width
    dma = pltpu.SemaphoreType.DMA
    peers, deep = max(plan.n_col - 1, 1), max(plan.deep - 1, 1)
    return [
        pltpu.VMEM((plan.total, width), F32), pltpu.VMEM((plan.total, width), BF),
        pltpu.VMEM((plan.half, width), BF), pltpu.VMEM((peers, plan.quarter, width), BF),
        pltpu.VMEM((deep, plan.small, width), BF), pltpu.VMEM((plan.half, width), BF),
        pltpu.VMEM((plan.total, width), BF), dma((4, 4)), dma((4, 4)),
        dma, dma, dma((peers,)), dma((peers,)), dma((deep,)), dma((deep,)),
        dma((deep,)), dma((deep,)), dma((peers,)), dma((peers,)), dma, dma]


def spread(local_bf, halo_bf, inverse, values, remote):
    summed = dot(local_bf, values) + values.astype(F32) + dot(halo_bf, remote)
    return (summed * inverse).astype(BF)


def retract(local_bf, halo_bf, inverse, upstream, weight, hits, returned):
    scaled = (dot(upstream, weight, ((1,), (1,))) * inverse).astype(BF)
    carried = dot(local_bf, scaled, ((0,), (0,))) + scaled.astype(F32) + dot(hits, returned)
    return carried, dot(halo_bf, scaled, ((0,), (0,))).astype(BF)


def per_device(mesh, features, local_mask, halo_mask, boundary_index, labels, halo_first, halo_second, halo_third,
               return_second, return_third, weight_first, weight_second, weight_third):
    features, local_mask, halo_mask = features[0, 0], local_mask[0, 0], halo_mask[0, 0]
    boundary_index, labels = boundary_index[0, 0], labels[0, 0]
    local_bf, halo_bf = local_mask.astype(BF), halo_mask.astype(BF)
    degree = 1.0 + jnp.sum(local_mask, axis=1).astype(F32) + jnp.sum(halo_mask, axis=1).astype(F32)
    inverse = (1.0 / degree)[:, None]
    nodes = features.shape[0]
    hits = (jnp.arange(nodes, dtype=jnp.int32)[:, None] == boundary_index[None, :]).astype(BF)
    mixed_one = spread(local_bf, halo_bf, inverse, features, halo_first[0, 0])
    pre_one = dot(mixed_one, weight_first)
    hidden_one = jax.nn.silu(pre_one).astype(BF)
    sent_second = dot(hits, hidden_one, ((0,), (0,))).astype(BF)
    mixed_two = spread(local_bf, halo_bf, inverse, hidden_one, halo_second[0, 0])
    pre_two = dot(mixed_two, weight_second)
    hidden_two = jax.nn.silu(pre_two).astype(BF)
    sent_third = dot(hits, hidden_two, ((0,), (0,))).astype(BF)
    mixed_three = spread(local_bf, halo_bf, inverse, hidden_two, halo_third[0, 0])
    logits = dot(mixed_three, weight_third)
    expo = jnp.exp(logits)
    probs = expo / jnp.sum(expo, axis=1, keepdims=True)
    target = (labels[:, None] == jnp.arange(logits.shape[1], dtype=jnp.int32)[None, :]).astype(F32)
    upstream_three = ((probs - target) / nodes).astype(BF)
    grad_three = dot(upstream_three, mixed_three, ((0,), (0,)))
    carried_two, outgoing_three = retract(local_bf, halo_bf, inverse, upstream_three, weight_third, hits, return_third[0, 0])
    upstream_two = (carried_two * slope(pre_two)).astype(BF)
    grad_two = dot(mixed_two, upstream_two, ((0,), (0,)))
    carried_one, outgoing_two = retract(local_bf, halo_bf, inverse, upstream_two, weight_second, hits, return_second[0, 0])
    upstream_one = (carried_one * slope(pre_one)).astype(BF)
    grad_one = dot(mixed_one, upstream_one, ((0,), (0,)))
    grads = (grad_one, grad_two, grad_three)
    plan = Plan(mesh, [g.shape[0] for g in grads], grad_one.shape[1])
    sent = (sent_second, sent_third, outgoing_two, outgoing_three)
    vmem = pl.BlockSpec(memory_space=pltpu.VMEM)
    done = pl.pallas_call(
        functools.partial(traffic, plan),
        out_shape=tuple(jax.ShapeDtypeStruct(v.shape, v.dtype) for v in grads + sent),
        in_specs=[vmem] * 7, out_specs=(vmem,) * 7, scratch_shapes=comm_scratch(plan),
        compiler_params=pltpu.CompilerParams(collective_id=0, has_side_effects=True),
        name="traffic",
    )(*grads, *sent)
    return (done[0], done[1], done[2].T) + tuple(v[None, None] for v in done[3:])


def solution(mesh):
    wide, flat, copied = P("row", "col", None, None), P("row", "col", None), P()
    return jax.shard_map(
        functools.partial(per_device, mesh), mesh=mesh,
        in_specs=(wide, wide, wide, flat, flat, wide, wide, wide, wide, wide, copied, copied, copied),
        out_specs=(copied, copied, copied, wide, wide, wide, wide),
        check_vma=False,
    )
```

```python
import functools

import jax
import jax.numpy as jnp
from jax import lax
from jax.experimental import pallas as pl
from jax.experimental.pallas import tpu as pltpu
from jax.sharding import PartitionSpec as P

MESH = pl.DeviceIdType.MESH
BF = jnp.bfloat16
F32 = jnp.float32


def up_to(value, step):
    return -(-value // step) * step


def dot(a, b, dims=((1,), (0,))):
    return lax.dot_general(a, b, (dims, ((), ())), preferred_element_type=F32)


def slope(pre):
    sigma = jax.nn.sigmoid(pre)
    return sigma * (1.0 + pre * (1.0 - sigma))


class Plan:
    def __init__(self, mesh, first, second, third):
        self.n_row, self.n_col = mesh.shape["row"], mesh.shape["col"]
        self.pair = 2 if self.n_row % 2 == 0 else 1
        self.deep = self.n_row // self.pair
        self.small = 16
        self.quarter = self.small * self.deep
        self.half = self.quarter * self.n_col
        self.piece = self.half * self.pair
        self.lanes = 128 if first[1] % 128 == 0 else first[1]
        self.strips = first[1] // self.lanes
        self.at_second = 0
        self.early = up_to(up_to(second[0], 16) * self.strips, self.piece) // self.piece
        self.at_first = self.early * self.piece
        self.at_third = self.at_first + up_to(first[0], 16) * self.strips
        self.pieces = up_to(self.at_third + up_to(third[0], 16) * self.strips, self.piece) // self.piece
        self.total = self.pieces * self.piece

    def strip(self, at, count, j):
        at = at + j * up_to(count, 16)
        return slice(at, at + count), slice(j * self.lanes, (j + 1) * self.lanes)

    def place(self):
        self.r, self.c = lax.axis_index("row"), lax.axis_index("col")
        self.core, self.z = self.r % self.pair, self.r // self.pair
        self.mate = self.r + 1 - 2 * self.core

    def col_peer(self, d):
        return (self.c + d) % self.n_col

    def deep_peer(self, d):
        return (self.z + d) % self.deep

    def deep_id(self, d):
        return (self.deep_peer(d) * self.pair + self.core, self.c)

    def greet(self):
        barrier = pltpu.get_barrier_semaphore()

        def hello(device):
            pl.semaphore_signal(barrier, inc=1, device_id=device, device_id_type=MESH)

        count = 0
        if self.pair == 2:
            hello((self.mate, self.c))
            count += 1
        for d in range(1, self.n_col):
            hello((self.r, self.col_peer(d)))
            count += 1
        for d in range(1, self.deep):
            hello(self.deep_id(d))
            count += 1
        for step, there in self.far_rows():
            @pl.when(there)
            def _():
                hello((self.r + step, self.c))
        for _, there in self.far_rows():
            count = count + jnp.where(there, 1, 0)
        pl.semaphore_wait(barrier, count)

    def far_rows(self):
        if self.pair == 2:
            return ((-1, jnp.logical_and(self.core == 0, self.r > 0)),
                    (1, jnp.logical_and(self.core == 1, self.r < self.n_row - 1)))
        return ()

    def edges(self):
        r, c = self.r, self.c
        return (((r - 1, c), 1, r > 0), ((r + 1, c), 0, r < self.n_row - 1),
                ((r, c - 1), 3, c > 0), ((r, c + 1), 2, c < self.n_col - 1))


def rows_at(start, count):
    return pl.ds(pl.multiple_of(start, 16), count)


def halo_copy(plan, k, src, dst, send, recv, way):
    bound = src.shape[0] // 4
    device, slot, there = plan.edges()[k]
    copy = pltpu.make_async_remote_copy(
        src_ref=src.at[pl.ds(k * bound, bound)], dst_ref=dst.at[pl.ds(slot * bound, bound)],
        send_sem=send.at[way, k], recv_sem=recv.at[way, slot], device_id=device, device_id_type=MESH)
    return copy, slot, there


def halo_start(plan, src, dst, send, recv, way):
    bound = src.shape[0] // 4
    for k in range(4):
        copy, _, there = halo_copy(plan, k, src, dst, send, recv, way)

        @pl.when(there)
        def _():
            copy.start()

        @pl.when(jnp.logical_not(there))
        def _():
            dst[pl.ds(k * bound, bound), :] = jnp.zeros((bound, dst.shape[1]), dst.dtype)


def halo_finish(plan, src, dst, send, recv, way):
    bound = src.shape[0] // 4
    for k in range(4):
        copy, _, there = halo_copy(plan, k, src, dst, send, recv, way)
        arrival = pltpu.make_async_remote_copy(
            src_ref=src.at[pl.ds(k * bound, bound)], dst_ref=dst.at[pl.ds(k * bound, bound)],
            send_sem=send.at[way, k], recv_sem=recv.at[way, k], device_id=plan.edges()[k][0], device_id_type=MESH)

        @pl.when(there)
        def _():
            copy.wait_send()
            arrival.wait_recv()


class Summer:
    STAGES = 6

    def __init__(self, plan, packed, packed_bf, got_pair, got_col, got_deep, acc_bf, whole, sems):
        self.plan, self.packed, self.packed_bf, self.whole = plan, packed, packed_bf, whole
        self.got_pair, self.got_col, self.got_deep, self.acc_bf = got_pair, got_col, got_deep, acc_bf
        self.sems = sems
        self.flying = {}
        self.stage = [0] * plan.pieces

    def copy(self, p, src, dst, kind, d, device):
        copy = pltpu.make_async_remote_copy(
            src_ref=src, dst_ref=dst, send_sem=self.sems[2 * kind].at[p, d], recv_sem=self.sems[2 * kind + 1].at[p, d],
            device_id=device, device_id_type=MESH)
        copy.start()
        self.flying[p].append(copy)

    def land(self, p):
        for copy in self.flying.get(p, ()):
            copy.wait()
        self.flying[p] = []

    def advance(self, p):
        plan, base = self.plan, p * self.plan.piece
        half, quarter, small = plan.half, plan.quarter, plan.small
        mine = base + plan.core * half
        own = mine + plan.c * quarter
        last = own + plan.z * small
        packed, whole, acc = self.packed, self.whole, self.acc_bf.at[p]
        stage = self.stage[p]
        self.stage[p] += 1
        self.land(p)
        if stage == 0 and plan.pair == 2:
            self.copy(p, self.packed_bf.at[rows_at(base + (1 - plan.core) * half, half)], self.got_pair.at[p], 0, 0, (plan.mate, plan.c))
        elif stage == 1:
            total = packed[rows_at(mine, half), :]
            if plan.pair == 2:
                total = total + self.got_pair[p].astype(F32)
            packed[rows_at(mine, half), :] = total
            acc[...] = total.astype(BF)
            for d in range(1, plan.n_col):
                peer = plan.col_peer(d)
                self.copy(p, acc.at[rows_at(peer * quarter, quarter)], self.got_col.at[p, d - 1], 1, d - 1, (plan.r, peer))
        elif stage == 2:
            total = packed[rows_at(own, quarter), :]
            for d in range(1, plan.n_col):
                total = total + self.got_col[p, d - 1].astype(F32)
            packed[rows_at(own, quarter), :] = total
            acc[0:quarter, :] = total.astype(BF)
            for d in range(1, plan.deep):
                self.copy(p, acc.at[rows_at(plan.deep_peer(d) * small, small)], self.got_deep.at[p, d - 1], 2, d - 1, plan.deep_id(d))
        elif stage == 3:
            total = packed[rows_at(last, small), :]
            for d in range(1, plan.deep):
                total = total + self.got_deep[p, d - 1].astype(F32)
            whole[rows_at(last, small), :] = total.astype(BF)
            part = whole.at[rows_at(last, small)]
            for d in range(1, plan.deep):
                self.copy(p, part, part, 3, d - 1, plan.deep_id(d))
        elif stage == 4:
            part = whole.at[rows_at(own, quarter)]
            for d in range(1, plan.n_col):
                self.copy(p, part, part, 4, d - 1, (plan.r, plan.col_peer(d)))
        elif stage == 5 and plan.pair == 2:
            part = whole.at[rows_at(mine, half)]
            self.copy(p, part, part, 5, 0, (plan.mate, plan.c))


NAMES = ("local", "halo", "features", "halo_first", "halo_second", "halo_third", "return_second", "return_third",
         "weight_first", "weight_second", "weight_third", "index_row", "index_col", "labels")


def step_kernel(plan, tiles, *refs):
    count = len(NAMES)
    hbm = dict(zip(NAMES, refs[:count]))
    whole, n2, n3, b2, b3 = refs[count:count + 5]
    held = dict(zip(NAMES, refs[count + 5:2 * count + 5]))
    (in_sem, local_bf, halo_bf, inverse, hits, hits_t, mixed_one, mixed_two, mixed_three, pre_one, pre_two, hidden_one,
     hidden_two, scaled, upstream, upstream_three, s2, s3, o2, o3, hsend, hrecv,
     packed, packed_bf, got_pair, got_col, got_deep, acc_bf) = refs[2 * count + 5:2 * count + 33]
    sems = refs[2 * count + 33:]
    nodes = held["features"].shape[0]
    tall = nodes // tiles
    tile = [pl.ds(t * tall, tall) for t in range(tiles)]
    plan.place()

    loads = {}
    for name in ("index_row", "index_col", "features", "halo_first", "local", "halo") + NAMES[4:11] + ("labels",):
        if name in ("local", "halo"):
            for t in range(tiles):
                key = (name, t)
                loads[key] = pltpu.make_async_copy(hbm[name].at[tile[t]], held[name].at[tile[t]], in_sem.at[len(loads)])
        else:
            loads[name] = pltpu.make_async_copy(hbm[name], held[name], in_sem.at[len(loads)])
    order = ["index_row", "index_col", "features", "halo_first"]
    for t in range(tiles):
        order += [("local", t), ("halo", t)]
    order += [name for name in loads if name not in order]
    for key in order:
        loads[key].start()

    plan.greet()
    packed[...] = jnp.zeros_like(packed)
    packed_bf[...] = jnp.zeros_like(packed_bf)
    summer = Summer(plan, packed, packed_bf, got_pair, got_col, got_deep, acc_bf, whole, sems)

    def put(value, at):
        for j in range(plan.strips):
            rows, lanes = plan.strip(at, value.shape[0], j)
            packed[rows, :] = value[:, lanes]
            packed_bf[rows, :] = value[:, lanes].astype(BF)

    loads["index_row"].wait()
    loads["index_col"].wait()
    slots = hits.shape[1]
    hits[...] = jnp.where(lax.broadcasted_iota(jnp.int32, (nodes, slots), 0) == held["index_row"][...], 1.0, 0.0).astype(BF)
    hits_t[...] = jnp.where(lax.broadcasted_iota(jnp.int32, (slots, nodes), 1) == held["index_col"][...], 1.0, 0.0).astype(BF)
    loads["features"].wait()
    loads["halo_first"].wait()

    def spread(t, values, remote, out):
        total = dot(local_bf[tile[t], :], values[...]) + values[tile[t], :].astype(F32) + dot(halo_bf[tile[t], :], remote[...])
        out[tile[t], :] = (total * inverse[tile[t], :]).astype(BF)

    for t in range(tiles):
        loads[("local", t)].wait()
        loads[("halo", t)].wait()
        near, far = held["local"][tile[t], :].astype(F32), held["halo"][tile[t], :].astype(F32)
        local_bf[tile[t], :] = near.astype(BF)
        halo_bf[tile[t], :] = far.astype(BF)
        inverse[tile[t], :] = 1.0 / (1.0 + jnp.sum(near, axis=1, keepdims=True) + jnp.sum(far, axis=1, keepdims=True))
        spread(t, held["features"], held["halo_first"], mixed_one)
        if t == 0:
            for name in NAMES[4:11] + ("labels",):
                loads[name].wait()
        pre = dot(mixed_one[tile[t], :], held["weight_first"][...])
        pre_one[tile[t], :] = pre
        hidden_one[tile[t], :] = (pre * jax.nn.sigmoid(pre)).astype(BF)
    s2[...] = dot(hits_t[...], hidden_one[...]).astype(BF)
    halo_start(plan, s2, n2, hsend, hrecv, 0)
    for t in range(tiles):
        spread(t, hidden_one, held["halo_second"], mixed_two)
        pre = dot(mixed_two[tile[t], :], held["weight_second"][...])
        pre_two[tile[t], :] = pre
        hidden_two[tile[t], :] = (pre * jax.nn.sigmoid(pre)).astype(BF)
    s3[...] = dot(hits_t[...], hidden_two[...]).astype(BF)
    halo_start(plan, s3, n3, hsend, hrecv, 1)
    for t in range(tiles):
        spread(t, hidden_two, held["halo_third"], mixed_three)
        logits = dot(mixed_three[tile[t], :], held["weight_third"][...])
        expo = jnp.exp(logits)
        probs = expo / jnp.sum(expo, axis=1, keepdims=True)
        target = jnp.where(held["labels"][tile[t], :] == lax.broadcasted_iota(jnp.int32, logits.shape, 1), 1.0, 0.0)
        up = ((probs - target) / nodes).astype(BF)
        upstream_three[tile[t], :] = up
        scaled[tile[t], :] = (dot(up, held["weight_third"][...], ((1,), (1,))) * inverse[tile[t], :]).astype(BF)
    turn = ((0,), (0,))

    def carry(t, returned):
        return dot(local_bf[:, tile[t]], scaled[...], turn) + scaled[tile[t], :].astype(F32) + dot(hits[tile[t], :], returned[...])

    for t in range(tiles):
        upstream[tile[t], :] = (carry(t, held["return_third"]) * slope(pre_two[tile[t], :])).astype(BF)
    put(dot(mixed_two[...], upstream[...], turn), plan.at_second)
    for p in range(plan.early):
        summer.advance(p)
    o3[...] = dot(halo_bf[...], scaled[...], turn).astype(BF)
    halo_start(plan, o3, b3, hsend, hrecv, 2)
    put(dot(upstream_three[...], mixed_three[...], turn), plan.at_third)
    for t in range(tiles):
        across = dot(upstream[tile[t], :], held["weight_second"][...], ((1,), (1,)))
        scaled[tile[t], :] = (across * inverse[tile[t], :]).astype(BF)
    for p in range(plan.early):
        summer.advance(p)
    for t in range(tiles):
        upstream[tile[t], :] = (carry(t, held["return_second"]) * slope(pre_one[tile[t], :])).astype(BF)
    for p in range(plan.early):
        summer.advance(p)
    put(dot(mixed_one[...], upstream[...], turn), plan.at_first)
    for p in range(plan.early, plan.pieces):
        summer.advance(p)
    for p in range(plan.early):
        summer.advance(p)
    o2[...] = dot(halo_bf[...], scaled[...], turn).astype(BF)
    halo_start(plan, o2, b2, hsend, hrecv, 3)
    for stage in range(1, Summer.STAGES):
        for p in list(range(plan.early, plan.pieces)) + list(range(plan.early)):
            if summer.stage[p] < Summer.STAGES:
                summer.advance(p)
    for p in range(plan.pieces):
        summer.land(p)
    for way, (src, dst) in enumerate(((s2, n2), (s3, n3), (o3, b3), (o2, b2))):
        halo_finish(plan, src, dst, hsend, hrecv, way)


def finish_kernel(plan, whole, n2, n3, b2, b3, g1, g2, g3, m2, m3, a2, a3, h1, h2, h3, sem):
    copies = [pltpu.make_async_copy(src, dst, sem.at[i]) for i, (src, dst) in enumerate(((n2, m2), (n3, m3), (b2, a2), (b3, a3)))]
    for copy in copies:
        copy.start()
    for ref, at in ((h1, plan.at_first), (h2, plan.at_second)):
        for j in range(plan.strips):
            rows, lanes = plan.strip(at, ref.shape[0], j)
            ref[:, lanes] = whole[rows, :].astype(F32)
    classes = h3.shape[1]
    for j in range(plan.strips):
        rows, lanes = plan.strip(plan.at_third, up_to(classes, 16), j)
        h3[lanes, :] = whole[rows, :].astype(F32).T[:, :classes]
    for i, (src, dst) in enumerate(((h1, g1), (h2, g2), (h3, g3))):
        copies.append(pltpu.make_async_copy(src, dst, sem.at[4 + i]))
        copies[-1].start()
    for copy in copies:
        copy.wait()


def per_device(mesh, features, local_mask, halo_mask, boundary_index, labels, halo_first, halo_second, halo_third,
               return_second, return_third, weight_first, weight_second, weight_third):
    features, local_mask, halo_mask = features[0, 0], local_mask[0, 0], halo_mask[0, 0]
    index, labels = boundary_index[0, 0], labels[0, 0]
    halo_first, halo_second, halo_third = halo_first[0, 0], halo_second[0, 0], halo_third[0, 0]
    return_second, return_third = return_second[0, 0], return_third[0, 0]
    nodes, width = features.shape
    slots, hidden, classes = index.shape[0], weight_first.shape[1], weight_third.shape[1]
    plan = Plan(mesh, weight_first.shape, weight_second.shape, weight_third.shape[::-1])
    tiles = 4 if nodes % 512 == 0 else 1
    values = (local_mask, halo_mask, features, halo_first, halo_second, halo_third, return_second, return_third,
              weight_first, weight_second, weight_third, index[None, :], index[:, None], labels[:, None])
    vmem, anywhere = pl.BlockSpec(memory_space=pltpu.VMEM), pl.BlockSpec(memory_space=pl.ANY)
    dma = pltpu.SemaphoreType.DMA
    peers, deep, n, lanes = max(plan.n_col - 1, 1), max(plan.deep - 1, 1), plan.pieces, plan.lanes
    block = jax.ShapeDtypeStruct((slots, hidden), BF)
    done = pl.pallas_call(
        functools.partial(step_kernel, plan, tiles),
        out_shape=(jax.ShapeDtypeStruct((plan.total, lanes), BF),) + (block,) * 4,
        in_specs=[anywhere] * len(values), out_specs=(vmem,) * 5,
        scratch_shapes=[pltpu.VMEM(v.shape, v.dtype) for v in values] + [
            dma((len(values) + 2 * tiles,)), pltpu.VMEM((nodes, nodes), BF), pltpu.VMEM((nodes, slots), BF), pltpu.VMEM((nodes, 1), F32),
            pltpu.VMEM((nodes, slots), BF), pltpu.VMEM((slots, nodes), BF),
            pltpu.VMEM((nodes, width), BF), pltpu.VMEM((nodes, hidden), BF), pltpu.VMEM((nodes, hidden), BF),
            pltpu.VMEM((nodes, hidden), F32), pltpu.VMEM((nodes, hidden), F32),
            pltpu.VMEM((nodes, hidden), BF), pltpu.VMEM((nodes, hidden), BF), pltpu.VMEM((nodes, hidden), BF),
            pltpu.VMEM((nodes, hidden), BF), pltpu.VMEM((nodes, classes), BF)]
        + [pltpu.VMEM((slots, hidden), BF)] * 4 + [dma((4, 4)), dma((4, 4)),
            pltpu.VMEM((plan.total, lanes), F32), pltpu.VMEM((plan.total, lanes), BF),
            pltpu.VMEM((n, plan.half, lanes), BF), pltpu.VMEM((n, peers, plan.quarter, lanes), BF),
            pltpu.VMEM((n, deep, plan.small, lanes), BF), pltpu.VMEM((n, plan.half, lanes), BF),
            dma((n, 1)), dma((n, 1)), dma((n, peers)), dma((n, peers)), dma((n, deep)), dma((n, deep)),
            dma((n, deep)), dma((n, deep)), dma((n, peers)), dma((n, peers)), dma((n, 1)), dma((n, 1))],
        compiler_params=pltpu.CompilerParams(collective_id=0, has_side_effects=True),
        name="step",
    )(*values)
    whole, n2, n3, b2, b3 = done
    grads = ((weight_first.shape, F32), (weight_second.shape, F32), (weight_third.shape, F32))
    out = pl.pallas_call(
        functools.partial(finish_kernel, plan),
        out_shape=tuple(jax.ShapeDtypeStruct(*g) for g in grads) + (block,) * 4,
        in_specs=[vmem] * 5, out_specs=(anywhere,) * 7,
        scratch_shapes=[pltpu.VMEM(*g) for g in grads] + [dma((7,))],
        name="finish",
    )(whole, n2, n3, b2, b3)
    return out[:3] + tuple(v[None, None] for v in out[3:])


def solution(mesh):
    wide, flat, copied = P("row", "col", None, None), P("row", "col", None), P()
    return jax.shard_map(
        functools.partial(per_device, mesh), mesh=mesh,
        in_specs=(wide, wide, wide, flat, flat, wide, wide, wide, wide, wide, copied, copied, copied),
        out_specs=(copied, copied, copied, wide, wide, wide, wide),
        check_vma=False,
    )
```

```python
import functools

import jax
import jax.numpy as jnp
from jax import lax
from jax.experimental import pallas as pl
from jax.experimental.pallas import tpu as pltpu
from jax.sharding import PartitionSpec as P

MESH = pl.DeviceIdType.MESH
BF = jnp.bfloat16
F32 = jnp.float32


def up_to(value, step):
    return -(-value // step) * step


def dot(a, b, dims=((1,), (0,))):
    return lax.dot_general(a, b, (dims, ((), ())), preferred_element_type=F32)


def slope(pre):
    sigma = jax.nn.sigmoid(pre)
    return sigma * (1.0 + pre * (1.0 - sigma))


class Plan:
    def __init__(self, mesh, first, second, third):
        self.n_row, self.n_col = mesh.shape["row"], mesh.shape["col"]
        self.pair = 2 if self.n_row % 2 == 0 else 1
        self.deep = self.n_row // self.pair
        self.small = 16
        self.quarter = self.small * self.deep
        self.half = self.quarter * self.n_col
        self.piece = self.half * self.pair
        self.lanes = 128 if first[1] % 128 == 0 else first[1]
        self.strips = first[1] // self.lanes
        self.at_second = 0
        self.early = up_to(up_to(second[0], 16) * self.strips, self.piece) // self.piece
        self.at_first = self.early * self.piece
        self.at_third = self.at_first + up_to(first[0], 16) * self.strips
        self.pieces = up_to(self.at_third + up_to(third[0], 16) * self.strips, self.piece) // self.piece
        self.total = self.pieces * self.piece

    def strip(self, at, count, j):
        at = at + j * up_to(count, 16)
        return slice(at, at + count), slice(j * self.lanes, (j + 1) * self.lanes)

    def place(self):
        self.r, self.c = lax.axis_index("row"), lax.axis_index("col")
        self.core, self.z = self.r % self.pair, self.r // self.pair
        self.mate = self.r + 1 - 2 * self.core

    def col_peer(self, d):
        return (self.c + d) % self.n_col

    def deep_peer(self, d):
        return (self.z + d) % self.deep

    def deep_id(self, d):
        return (self.deep_peer(d) * self.pair + self.core, self.c)

    def greet(self):
        barrier = pltpu.get_barrier_semaphore()

        def hello(device):
            pl.semaphore_signal(barrier, inc=1, device_id=device, device_id_type=MESH)

        count = 0
        if self.pair == 2:
            hello((self.mate, self.c))
            count += 1
        for d in range(1, self.n_col):
            hello((self.r, self.col_peer(d)))
            count += 1
        for d in range(1, self.deep):
            hello(self.deep_id(d))
            count += 1
        for step, there in self.far_rows():
            @pl.when(there)
            def _():
                hello((self.r + step, self.c))
        for _, there in self.far_rows():
            count = count + jnp.where(there, 1, 0)
        pl.semaphore_wait(barrier, count)

    def far_rows(self):
        if self.pair == 2:
            return ((-1, jnp.logical_and(self.core == 0, self.r > 0)),
                    (1, jnp.logical_and(self.core == 1, self.r < self.n_row - 1)))
        return ()

    def edges(self):
        r, c = self.r, self.c
        return (((r - 1, c), 1, r > 0), ((r + 1, c), 0, r < self.n_row - 1),
                ((r, c - 1), 3, c > 0), ((r, c + 1), 2, c < self.n_col - 1))


def rows_at(start, count):
    return pl.ds(pl.multiple_of(start, 16), count)


def halo_copy(plan, k, src, dst, send, recv, way):
    bound = src.shape[0] // 4
    device, slot, there = plan.edges()[k]
    copy = pltpu.make_async_remote_copy(
        src_ref=src.at[pl.ds(k * bound, bound)], dst_ref=dst.at[pl.ds(slot * bound, bound)],
        send_sem=send.at[way, k], recv_sem=recv.at[way, slot], device_id=device, device_id_type=MESH)
    return copy, slot, there


def halo_start(plan, src, dst, send, recv, way):
    bound = src.shape[0] // 4
    for k in range(4):
        copy, _, there = halo_copy(plan, k, src, dst, send, recv, way)

        @pl.when(there)
        def _():
            copy.start()

        @pl.when(jnp.logical_not(there))
        def _():
            dst[pl.ds(k * bound, bound), :] = jnp.zeros((bound, dst.shape[1]), dst.dtype)


def halo_finish(plan, src, dst, send, recv, way):
    bound = src.shape[0] // 4
    for k in range(4):
        copy, _, there = halo_copy(plan, k, src, dst, send, recv, way)
        arrival = pltpu.make_async_remote_copy(
            src_ref=src.at[pl.ds(k * bound, bound)], dst_ref=dst.at[pl.ds(k * bound, bound)],
            send_sem=send.at[way, k], recv_sem=recv.at[way, k], device_id=plan.edges()[k][0], device_id_type=MESH)

        @pl.when(there)
        def _():
            copy.wait_send()
            arrival.wait_recv()


class Summer:
    STAGES = 6

    def __init__(self, plan, packed, packed_bf, got_pair, got_col, got_deep, acc_bf, whole, sems):
        self.plan, self.packed, self.packed_bf, self.whole = plan, packed, packed_bf, whole
        self.got_pair, self.got_col, self.got_deep, self.acc_bf = got_pair, got_col, got_deep, acc_bf
        self.sems = sems
        self.flying = {}
        self.stage = [0] * plan.pieces

    def copy(self, p, src, dst, kind, d, device):
        copy = pltpu.make_async_remote_copy(
            src_ref=src, dst_ref=dst, send_sem=self.sems[2 * kind].at[p, d], recv_sem=self.sems[2 * kind + 1].at[p, d],
            device_id=device, device_id_type=MESH)
        copy.start()
        self.flying[p].append(copy)

    def land(self, p):
        for copy in self.flying.get(p, ()):
            copy.wait()
        self.flying[p] = []

    def advance(self, p):
        plan, base = self.plan, p * self.plan.piece
        half, quarter, small = plan.half, plan.quarter, plan.small
        mine = base + plan.core * half
        own = mine + plan.c * quarter
        last = own + plan.z * small
        packed, whole, acc = self.packed, self.whole, self.acc_bf.at[p]
        stage = self.stage[p]
        self.stage[p] += 1
        self.land(p)
        if stage == 0 and plan.pair == 2:
            self.copy(p, self.packed_bf.at[rows_at(base + (1 - plan.core) * half, half)], self.got_pair.at[p], 0, 0, (plan.mate, plan.c))
        elif stage == 1:
            total = packed[rows_at(mine, half), :]
            if plan.pair == 2:
                total = total + self.got_pair[p].astype(F32)
            packed[rows_at(mine, half), :] = total
            acc[...] = total.astype(BF)
            for d in range(1, plan.n_col):
                peer = plan.col_peer(d)
                self.copy(p, acc.at[rows_at(peer * quarter, quarter)], self.got_col.at[p, d - 1], 1, d - 1, (plan.r, peer))
        elif stage == 2:
            total = packed[rows_at(own, quarter), :]
            for d in range(1, plan.n_col):
                total = total + self.got_col[p, d - 1].astype(F32)
            packed[rows_at(own, quarter), :] = total
            acc[0:quarter, :] = total.astype(BF)
            for d in range(1, plan.deep):
                self.copy(p, acc.at[rows_at(plan.deep_peer(d) * small, small)], self.got_deep.at[p, d - 1], 2, d - 1, plan.deep_id(d))
        elif stage == 3:
            total = packed[rows_at(last, small), :]
            for d in range(1, plan.deep):
                total = total + self.got_deep[p, d - 1].astype(F32)
            whole[rows_at(last, small), :] = total.astype(BF)
            part = whole.at[rows_at(last, small)]
            for d in range(1, plan.deep):
                self.copy(p, part, part, 3, d - 1, plan.deep_id(d))
        elif stage == 4:
            part = whole.at[rows_at(own, quarter)]
            for d in range(1, plan.n_col):
                self.copy(p, part, part, 4, d - 1, (plan.r, plan.col_peer(d)))
        elif stage == 5 and plan.pair == 2:
            part = whole.at[rows_at(mine, half)]
            self.copy(p, part, part, 5, 0, (plan.mate, plan.c))


NAMES = ("local", "halo", "features", "halo_first", "halo_second", "halo_third", "return_second", "return_third",
         "weight_first", "weight_second", "weight_third", "index_row", "labels")


def step_kernel(plan, tiles, *refs):
    count = len(NAMES)
    hbm = dict(zip(NAMES, refs[:count]))
    whole, n2, n3, b2, b3 = refs[count:count + 5]
    held = dict(zip(NAMES, refs[count + 5:2 * count + 5]))
    (in_sem, local_bf, halo_bf, inverse, hits, hits_t, mixed_one, mixed_two, mixed_three, pre_one, pre_two, hidden_one,
     hidden_two, scaled, upstream, upstream_three, target_held, s2, s3, o2, o3, hsend, hrecv,
     packed, packed_bf, got_pair, got_col, got_deep, acc_bf) = refs[2 * count + 5:2 * count + 34]
    sems = refs[2 * count + 34:]
    nodes = held["local"].shape[0]
    tall = nodes // tiles
    tile = [pl.ds(t * tall, tall) for t in range(tiles)]
    plan.place()

    loads = {}
    for name in ("index_row", "features", "halo_first", "local", "halo") + NAMES[4:11] + ("labels",):
        if name in ("local", "halo"):
            for t in range(tiles):
                key = (name, t)
                loads[key] = pltpu.make_async_copy(hbm[name].at[tile[t]], held[name].at[tile[t]], in_sem.at[len(loads)])
        else:
            loads[name] = pltpu.make_async_copy(hbm[name], held[name], in_sem.at[len(loads)])
    order = ["index_row", "features", "halo_first"]
    for t in range(tiles):
        order += [("local", t), ("halo", t)]
    order += [name for name in loads if name not in order]
    for key in order:
        loads[key].start()

    plan.greet()
    packed[...] = jnp.zeros_like(packed)
    packed_bf[...] = jnp.zeros_like(packed_bf)
    summer = Summer(plan, packed, packed_bf, got_pair, got_col, got_deep, acc_bf, whole, sems)

    def put(value, at):
        for j in range(plan.strips):
            rows, lanes = plan.strip(at, value.shape[0], j)
            packed[rows, :] = value[:, lanes]
            packed_bf[rows, :] = value[:, lanes].astype(BF)

    loads["index_row"].wait()
    slots = hits.shape[1]
    hits[...] = jnp.where(lax.broadcasted_iota(jnp.int32, (nodes, slots), 0) == held["index_row"][...], 1.0, 0.0).astype(BF)
    hits_t[...] = hits[...].T
    loads["labels"].wait()
    wide = target_held.shape[1]
    target_held[...] = jnp.where(lax.broadcasted_iota(jnp.int32, (wide, nodes), 0) == held["labels"][...], 1.0, 0.0).T
    loads["features"].wait()
    loads["halo_first"].wait()

    def spread(t, values, remote, out, dims=((1,), (0,))):
        total = dot(local_bf[tile[t], :], values[...], dims) + dot(halo_bf[tile[t], :], remote[...], dims)
        out[tile[t], :] = (total * inverse[tile[t], :]).astype(BF)

    for t in range(tiles):
        loads[("local", t)].wait()
        loads[("halo", t)].wait()
        near, far = held["local"][tile[t], :].astype(F32), held["halo"][tile[t], :].astype(F32)
        here = lax.broadcasted_iota(jnp.int32, near.shape, 0) + t * tall == lax.broadcasted_iota(jnp.int32, near.shape, 1)
        local_bf[tile[t], :] = jnp.where(here, near + 1.0, near).astype(BF)
        halo_bf[tile[t], :] = far.astype(BF)
        inverse[tile[t], :] = 1.0 / (1.0 + jnp.sum(near, axis=1, keepdims=True) + jnp.sum(far, axis=1, keepdims=True))
        spread(t, held["features"], held["halo_first"], mixed_one, ((1,), (1,)))
        if t == 0:
            for name in NAMES[4:11]:
                loads[name].wait()
        pre = dot(mixed_one[tile[t], :], held["weight_first"][...])
        pre_one[tile[t], :] = pre
        hidden_one[tile[t], :] = (pre * jax.nn.sigmoid(pre)).astype(BF)
    s2[...] = dot(hits_t[...], hidden_one[...]).astype(BF)
    halo_start(plan, s2, n2, hsend, hrecv, 0)
    for t in range(tiles):
        spread(t, hidden_one, held["halo_second"], mixed_two)
        pre = dot(mixed_two[tile[t], :], held["weight_second"][...])
        pre_two[tile[t], :] = pre
        hidden_two[tile[t], :] = (pre * jax.nn.sigmoid(pre)).astype(BF)
    s3[...] = dot(hits_t[...], hidden_two[...]).astype(BF)
    halo_start(plan, s3, n3, hsend, hrecv, 1)
    for t in range(tiles):
        spread(t, hidden_two, held["halo_third"], mixed_three)
        logits = dot(mixed_three[tile[t], :], held["weight_third"][...], ((1,), (1,)))
        expo = jnp.exp(logits)
        probs = expo / jnp.sum(expo, axis=1, keepdims=True)
        target = target_held[tile[t], :logits.shape[1]]
        up = ((probs - target) / nodes).astype(BF)
        upstream_three[tile[t], :] = up
        scaled[tile[t], :] = (dot(up, held["weight_third"][...]) * inverse[tile[t], :]).astype(BF)
    turn = ((0,), (0,))

    def carry(t, returned):
        return dot(local_bf[:, tile[t]], scaled[...], turn) + dot(hits[tile[t], :], returned[...])

    for t in range(tiles):
        upstream[tile[t], :] = (carry(t, held["return_third"]) * slope(pre_two[tile[t], :])).astype(BF)
    put(dot(mixed_two[...], upstream[...], turn), plan.at_second)
    for p in range(plan.early):
        summer.advance(p)
    o3[...] = dot(halo_bf[...], scaled[...], turn).astype(BF)
    halo_start(plan, o3, b3, hsend, hrecv, 2)
    put(dot(upstream_three[...], mixed_three[...], turn), plan.at_third)
    for t in range(tiles):
        across = dot(upstream[tile[t], :], held["weight_second"][...], ((1,), (1,)))
        scaled[tile[t], :] = (across * inverse[tile[t], :]).astype(BF)
    for p in range(plan.early):
        summer.advance(p)
    for t in range(tiles):
        upstream[tile[t], :] = (carry(t, held["return_second"]) * slope(pre_one[tile[t], :])).astype(BF)
    for p in range(plan.early):
        summer.advance(p)
    put(dot(mixed_one[...], upstream[...], turn), plan.at_first)
    for p in range(plan.early, plan.pieces):
        summer.advance(p)
    for p in range(plan.early):
        summer.advance(p)
    o2[...] = dot(halo_bf[...], scaled[...], turn).astype(BF)
    halo_start(plan, o2, b2, hsend, hrecv, 3)
    for stage in range(1, Summer.STAGES):
        for p in list(range(plan.early, plan.pieces)) + list(range(plan.early)):
            if summer.stage[p] < Summer.STAGES:
                summer.advance(p)
    for p in range(plan.pieces):
        summer.land(p)
    for way, (src, dst) in enumerate(((s2, n2), (s3, n3), (o3, b3), (o2, b2))):
        halo_finish(plan, src, dst, hsend, hrecv, way)


def finish_kernel(plan, whole, n2, n3, b2, b3, g1, g2, g3, m2, m3, a2, a3, h1, h2, h3, sem):
    copies = [pltpu.make_async_copy(src, dst, sem.at[i]) for i, (src, dst) in enumerate(((n2, m2), (n3, m3), (b2, a2), (b3, a3)))]
    for copy in copies:
        copy.start()
    for ref, at in ((h1, plan.at_first), (h2, plan.at_second), (h3, plan.at_third)):
        for j in range(plan.strips):
            rows, lanes = plan.strip(at, ref.shape[0], j)
            ref[:, lanes] = whole[rows, :].astype(F32)
    for i, (src, dst) in enumerate(((h1, g1), (h2, g2), (h3, g3))):
        copies.append(pltpu.make_async_copy(src, dst, sem.at[4 + i]))
        copies[-1].start()
    for copy in copies:
        copy.wait()


def per_device(mesh, features, local_mask, halo_mask, boundary_index, labels, halo_first, halo_second, halo_third,
               return_second, return_third, weight_first, weight_second, weight_third):
    features, local_mask, halo_mask = features[0, 0], local_mask[0, 0], halo_mask[0, 0]
    index, labels = boundary_index[0, 0], labels[0, 0]
    halo_first, halo_second, halo_third = halo_first[0, 0], halo_second[0, 0], halo_third[0, 0]
    return_second, return_third = return_second[0, 0], return_third[0, 0]
    nodes, width = features.shape
    slots, hidden, classes = index.shape[0], weight_first.shape[1], weight_third.shape[1]
    plan = Plan(mesh, weight_first.shape, weight_second.shape, weight_third.shape[::-1])
    tiles = 4 if nodes % 512 == 0 else 1
    values = (local_mask, halo_mask, features.T, halo_first.T, halo_second, halo_third, return_second, return_third,
              weight_first, weight_second, weight_third.T, index[None, :], labels[None, :])
    vmem, anywhere = pl.BlockSpec(memory_space=pltpu.VMEM), pl.BlockSpec(memory_space=pl.ANY)
    dma = pltpu.SemaphoreType.DMA
    peers, deep, n, lanes = max(plan.n_col - 1, 1), max(plan.deep - 1, 1), plan.pieces, plan.lanes
    block = jax.ShapeDtypeStruct((slots, hidden), BF)
    done = pl.pallas_call(
        functools.partial(step_kernel, plan, tiles),
        out_shape=(jax.ShapeDtypeStruct((plan.total, lanes), BF),) + (block,) * 4,
        in_specs=[anywhere] * len(values), out_specs=(vmem,) * 5,
        scratch_shapes=[pltpu.VMEM(v.shape, v.dtype) for v in values] + [
            dma((len(values) + 2 * tiles,)), pltpu.VMEM((nodes, nodes), BF), pltpu.VMEM((nodes, slots), BF), pltpu.VMEM((nodes, 1), F32),
            pltpu.VMEM((nodes, slots), BF), pltpu.VMEM((slots, nodes), BF),
            pltpu.VMEM((nodes, width), BF), pltpu.VMEM((nodes, hidden), BF), pltpu.VMEM((nodes, hidden), BF),
            pltpu.VMEM((nodes, hidden), F32), pltpu.VMEM((nodes, hidden), F32),
            pltpu.VMEM((nodes, hidden), BF), pltpu.VMEM((nodes, hidden), BF), pltpu.VMEM((nodes, hidden), BF),
            pltpu.VMEM((nodes, hidden), BF), pltpu.VMEM((nodes, classes), BF),
            pltpu.VMEM((nodes, up_to(classes, 128)), F32)]
        + [pltpu.VMEM((slots, hidden), BF)] * 4 + [dma((4, 4)), dma((4, 4)),
            pltpu.VMEM((plan.total, lanes), F32), pltpu.VMEM((plan.total, lanes), BF),
            pltpu.VMEM((n, plan.half, lanes), BF), pltpu.VMEM((n, peers, plan.quarter, lanes), BF),
            pltpu.VMEM((n, deep, plan.small, lanes), BF), pltpu.VMEM((n, plan.half, lanes), BF),
            dma((n, 1)), dma((n, 1)), dma((n, peers)), dma((n, peers)), dma((n, deep)), dma((n, deep)),
            dma((n, deep)), dma((n, deep)), dma((n, peers)), dma((n, peers)), dma((n, 1)), dma((n, 1))],
        compiler_params=pltpu.CompilerParams(collective_id=0, has_side_effects=True),
        name="step",
    )(*values)
    whole, n2, n3, b2, b3 = done
    grads = ((weight_first.shape, F32), (weight_second.shape, F32), (weight_third.shape[::-1], F32))
    out = pl.pallas_call(
        functools.partial(finish_kernel, plan),
        out_shape=tuple(jax.ShapeDtypeStruct(*g) for g in grads) + (block,) * 4,
        in_specs=[vmem] * 5, out_specs=(anywhere,) * 7,
        scratch_shapes=[pltpu.VMEM(*g) for g in grads] + [dma((7,))],
        name="finish",
    )(whole, n2, n3, b2, b3)
    return (out[0], out[1], out[2].T) + tuple(v[None, None] for v in out[3:])


def solution(mesh):
    wide, flat, copied = P("row", "col", None, None), P("row", "col", None), P()
    return jax.shard_map(
        functools.partial(per_device, mesh), mesh=mesh,
        in_specs=(wide, wide, wide, flat, flat, wide, wide, wide, wide, wide, copied, copied, copied),
        out_specs=(copied, copied, copied, wide, wide, wide, wide),
        check_vma=False,
    )
```
